256 devices in a mesh: blk: 8 (over y, x_hi), ctx: 32 (over z, x_lo, core).
Axes of the slice: x: 4 (x_hi: 2, x_lo: 2; x = x_hi * 2 + x_lo), y: 4, z: 8, core: 2. Of those that a mesh axis runs over, the one named last changes fastest.
Arguments:
- tokens: bfloat16 [8, 4096, 1024], P('blk', 'ctx'), may hold values from -16 to 16
- segment_ids: int32 [8, 4096], P('blk', 'ctx'), may hold values from 0 to 3, never falling along the last dimension, each value on 1 to 3072 neighbouring positions
- norm_gain: bfloat16 [8, 2, 1024], P('blk'), may hold values from 0.25 to 1.75
- w_mamba_in: bfloat16 [8, 1024, 2048], P('blk', None, 'ctx'), may hold values from -0.1875 to 0.1875
- w_ssm_param: bfloat16 [8, 1024, 160], P('blk'), may hold values from -0.1875 to 0.1875
- ssm_rate: bfloat16 [8, 32], P('blk'), may hold values from 7.2956085e-05 to 0.059814453
- dt_bias: bfloat16 [8, 32], P('blk'), may hold values from -1 to 1
- skip_gain: bfloat16 [8, 32], P('blk'), may hold values from 0.5 to 1.5
- ssm_norm_gain: bfloat16 [8, 2048], P('blk'), may hold values from 0.25 to 1.75
- w_mamba_out: bfloat16 [8, 2048, 1024], P('blk', 'ctx'), may hold values from -0.125 to 0.125
- w_qkv: bfloat16 [8, 1024, 2048], P('blk', None, 'ctx'), may hold values from -1.5 to 1.5
- w_attn_out: bfloat16 [8, 1024, 1024], P('blk', 'ctx'), may hold values from -0.75 to 0.75
Outputs:
- layer_out: bfloat16 [8, 4096, 1024], P('blk', 'ctx')
The draws below stay inside these ranges and needn't reach their ends.
Inputs may be any that keep to these rules, and one draw needn't show every extreme that they name: `segment_ids`: within each micro-batch the ids never fall along the sequence; each document holds 1 to 3072 tokens, and one holds exactly that many.
All inputs are finite; a program needn't handle non-finite values.
Results may differ from the reference program's by a relative error of at most 0.015.
Values may be sent and summed in bfloat16 or wider, within the bound.
No kernel may reach another device: no remote copies, remote signals or barrier semaphores. Data moves between devices by JAX's collectives and lax.ppermute only.
A program may use at most 128 MiB of HBM per device.

```python
import math
import jax
import jax.numpy as jnp
import numpy as np
from jax import lax

MODEL = 1024
INNER = 2048
HEAD_DIM = 64
STATE = 64
QUERY_HEADS = 8
KV_HEADS = 4
ATTN_DIM = 128
SPAN = 64
SSM_HEADS = 32
SECTIONS = 8
LENGTH = 4096


def draw_tokens(key, part):
    base = jax.random.normal(jax.random.fold_in(key, 7011), (SECTIONS, LENGTH, MODEL), jnp.float32)
    return jnp.clip(base, -6.0, 6.0).astype(jnp.bfloat16)


def draw_w_qkv(key, part):
    columns = (QUERY_HEADS + 2 * KV_HEADS) * ATTN_DIM
    base = jax.random.normal(jax.random.fold_in(key, 7021), (SECTIONS, MODEL, columns), jnp.float32) / math.sqrt(MODEL)
    return jnp.clip(base, -1.5, 1.5).astype(jnp.bfloat16)


def block_scale(key, extent, pieces, smallest, high):
    def one(dim, parts):
        steps = jax.random.uniform(jax.random.fold_in(jax.random.fold_in(key, 6), dim), (parts,), jnp.float32, smallest / len(pieces), high / len(pieces))
        return jnp.repeat(jnp.exp(steps), extent[dim] // parts).reshape((-1,) + (1,) * (len(extent) - dim - 1))

    level = one(*pieces[0])
    for cut in pieces[1:]:
        level = level * one(*cut)
    return level


def length_profile(amount, total, most, slope):
    weights = [(1 << 20) // math.isqrt(grade ** slope) + 1 for grade in range(2, amount + 1)]
    spare, holding = total - most - (amount - 1), [1] * (amount - 1)
    while spare > 0:
        candidates = [i for i in range(amount - 1) if holding[i] < most]
        whole, budget = sum([weights[i] for i in candidates]), spare
        for i in candidates:
            extra = min(most - holding[i], max(1, budget * weights[i] // whole), spare)
            holding[i] = holding[i] + extra
            spare = spare - extra
    return np.array([most] + holding)


def uneven(key, count, total, bound, lean):
    if count == 2:
        one = jax.random.randint(key, (), max(1, total - bound), min(bound, total - 1) + 1)
        return jnp.stack([one, total - one])
    tallies = jnp.asarray(length_profile(count, total, bound, lean), jnp.int32)
    pairs = (count - 1) // 2
    giver, taker = tallies[1:1 + 2 * pairs:2], tallies[2:2 + 2 * pairs:2]
    room = jnp.minimum(giver - 1, bound - taker)
    shifted = jax.random.randint(jax.random.fold_in(key, 1), (pairs,), 0, 1 << 20) % (room + 1)
    tallies = tallies.at[1:1 + 2 * pairs:2].set(giver - shifted).at[2:2 + 2 * pairs:2].set(taker + shifted)
    return tallies[jax.random.permutation(jax.random.fold_in(key, 2), count)]


def noise(own_key, dims, deviation, limit, split=(), kind=jnp.bfloat16):
    values = jax.random.normal(own_key, dims, jnp.float32) * deviation
    if len(split) > 0:
        values = block_scale(own_key, dims, split, -0.22, 0.18) * values
    return jnp.clip(values, min=-limit, max=limit).astype(kind)


def setup_inputs(seed: int = 0) -> dict:
    key_of = jax.random.split(jax.random.key(seed), 13)
    return {
        "tokens": draw_tokens(jax.random.fold_in(key_of[12], 71), 0),
        "segment_ids": jax.vmap(lambda own: jnp.searchsorted(jnp.cumsum(uneven(own, 4, LENGTH, 3 * LENGTH // 4, 1)), jnp.arange(LENGTH), side="right"))(jax.random.split(key_of[1], SECTIONS)).reshape((SECTIONS, LENGTH)).astype(jnp.int32),
        "norm_gain": jnp.clip(1.0 + 0.15 * jax.random.normal(key_of[2], (SECTIONS, 2, MODEL), jnp.float32), 0.25, 1.75).astype(jnp.bfloat16),
        "w_mamba_in": noise(key_of[3], (SECTIONS, MODEL, INNER), MODEL ** -0.5, 0.1875, ((0, 8), (2, 32))),
        "w_ssm_param": noise(key_of[4], (SECTIONS, MODEL, 2 * STATE + SSM_HEADS), MODEL ** -0.5, 0.1875, ((0, 8),)),
        "ssm_rate": jnp.clip(jnp.exp(math.log(0.059814453) - 6.709145 * jax.random.uniform(key_of[5], (SECTIONS, SSM_HEADS), jnp.float32) ** block_scale(key_of[5], (SECTIONS, SSM_HEADS), ((0, 8),), -0.2, 0.2)), 7.295608520507812e-05, 0.059814453).astype(jnp.bfloat16),
        "dt_bias": jnp.clip(jax.random.uniform(key_of[6], (SECTIONS, SSM_HEADS), jnp.float32, -1.0, 1.0) * block_scale(key_of[6], (SECTIONS, SSM_HEADS), ((0, 8),), -0.4, 0.0), -1.0, 1.0).astype(jnp.bfloat16),
        "skip_gain": jnp.clip(0.5 + 1.0 * jax.random.uniform(key_of[7], (SECTIONS, SSM_HEADS), jnp.float32) ** block_scale(key_of[7], (SECTIONS, SSM_HEADS), ((0, 8),), -0.2, 0.2), 0.5, 1.5).astype(jnp.bfloat16),
        "ssm_norm_gain": jnp.clip(1.0 + 0.15 * jax.random.normal(key_of[8], (SECTIONS, INNER), jnp.float32), 0.25, 1.75).astype(jnp.bfloat16),
        "w_mamba_out": noise(key_of[9], (SECTIONS, INNER, MODEL), INNER ** -0.5, 0.125, ((0, 8), (1, 32))),
        "w_qkv": draw_w_qkv(jax.random.fold_in(key_of[12], 71), 0),
        "w_attn_out": noise(key_of[11], (SECTIONS, QUERY_HEADS * ATTN_DIM, MODEL), (QUERY_HEADS * ATTN_DIM // 16) ** -0.5, 0.75, ((0, 8), (1, 32))),
    }


epsilon = 1e-05
highest = lax.Precision.HIGHEST

def rms_norm(values, gain):
    values = values.astype(jnp.float32)
    scale = lax.rsqrt(lax.optimization_barrier(jnp.mean(values * values, axis=-1, keepdims=True)) + epsilon)
    return values * scale * gain.astype(jnp.float32)

def span_update(carry, block):
    state, prev_segment = carry
    inner_value, bin_value, cout_value, delta, log_decay, segment = block
    cumul = jnp.cumsum(log_decay, axis=0)
    order = jnp.arange(segment.shape[0])
    allowed = (order[:, None] >= order[None, :]) & (segment[:, None] == segment[None, :])
    differ = cumul[:, None, :] - cumul[None, :, :]
    factor = jnp.where(allowed[:, :, None], jnp.exp(jnp.minimum(differ, 0.0)), 0.0)
    intersection = jnp.dot(cout_value, bin_value.T, precision=highest)
    mixing = factor * intersection[:, :, None] * delta[None, :, :]
    within = jnp.einsum('tsh,shp->thp', mixing, inner_value, precision=highest)
    carried = jnp.where((segment == prev_segment)[:, None], jnp.exp(cumul), 0.0)
    across = jnp.einsum('tn,hpn->thp', cout_value, state, precision=highest) * carried[:, :, None]
    last_segment = segment[-1]
    keeping = jnp.where((segment == last_segment)[:, None], jnp.exp(cumul[-1][None, :] - cumul), 0.0) * delta
    fresh = jnp.einsum('sh,shp,sn->hpn', keeping, inner_value, bin_value, precision=highest)
    passing = jnp.where(prev_segment == last_segment, jnp.exp(cumul[-1]), 0.0)
    state = passing[:, None, None] * state + fresh
    return ((state, last_segment), within + across)

def micro_batch(tokens, segment, norm_gain, w_mamba_in, w_ssm_param, ssm_rate, dt_bias, skip_gain, ssm_norm_gain, w_mamba_out, w_qkv, w_attn_out):
    length = tokens.shape[0]
    heads = SSM_HEADS
    normed = rms_norm(tokens, norm_gain[0]).astype(jnp.bfloat16)
    inner = jnp.dot(normed, w_mamba_in, preferred_element_type=jnp.float32).astype(jnp.bfloat16)
    params = jnp.dot(normed, w_ssm_param, preferred_element_type=jnp.float32)
    bin_value = params[:, :STATE]
    cout_value = params[:, STATE:2 * STATE]
    delta = jax.nn.softplus(params[:, 2 * STATE:] + dt_bias.astype(jnp.float32))
    log_decay = -delta * ssm_rate.astype(jnp.float32)
    inner_value = inner.astype(jnp.float32).reshape(length, heads, HEAD_DIM)
    blocks = tuple((item.reshape((length // SPAN, SPAN) + item.shape[1:]) for item in (inner_value, bin_value, cout_value, delta, log_decay, segment)))
    start_carry = (jnp.zeros((heads, HEAD_DIM, STATE), jnp.float32), jnp.array(-1, jnp.int32))
    ignored, mixed = lax.scan(span_update, start_carry, blocks)
    mixed = mixed.reshape(length, heads, HEAD_DIM) + skip_gain.astype(jnp.float32)[None, :, None] * inner_value
    ssm_out = rms_norm(mixed.reshape(length, INNER), ssm_norm_gain).astype(jnp.bfloat16)
    first = tokens.astype(jnp.float32) + jnp.dot(ssm_out, w_mamba_out, preferred_element_type=jnp.float32)
    hidden = rms_norm(first, norm_gain[1]).astype(jnp.bfloat16)
    projected = jnp.dot(hidden, w_qkv, preferred_element_type=jnp.float32).astype(jnp.bfloat16)
    groups = QUERY_HEADS // KV_HEADS
    query = projected[:, :QUERY_HEADS * ATTN_DIM].reshape(length, KV_HEADS, groups, ATTN_DIM).astype(jnp.float32)
    keys = projected[:, QUERY_HEADS * ATTN_DIM:(QUERY_HEADS + KV_HEADS) * ATTN_DIM].reshape(length, KV_HEADS, ATTN_DIM).astype(jnp.float32)
    values = projected[:, (QUERY_HEADS + KV_HEADS) * ATTN_DIM:].reshape(length, KV_HEADS, ATTN_DIM).astype(jnp.float32)
    positions = jnp.arange(length)
    width = math.gcd(512, length)
    scale = 1.0 / math.sqrt(ATTN_DIM)

    def attend(block_index):
        begin = block_index * width
        query_block = lax.dynamic_slice_in_dim(query, begin, width, 0)
        query_segment = lax.dynamic_slice_in_dim(segment, begin, width, 0)
        query_position = begin + jnp.arange(width)
        scores = jnp.einsum('tkgd,skd->kgts', query_block, keys, precision=highest) * scale
        allowed = (positions[None, :] <= query_position[:, None]) & (segment[None, :] == query_segment[:, None])
        scores = jnp.where(allowed, scores, -1e+30)
        top = lax.optimization_barrier(jnp.max(scores, axis=-1, keepdims=True))
        probs = jnp.where(allowed, jnp.exp(scores - top), 0.0)
        total = lax.optimization_barrier(jnp.sum(probs, axis=-1))
        rounded = probs.astype(jnp.bfloat16).astype(jnp.float32)
        context = jnp.einsum('kgts,skd->kgtd', rounded, values, precision=highest) / total[..., None]
        return jnp.transpose(context, (2, 0, 1, 3)).reshape(width, QUERY_HEADS * ATTN_DIM).astype(jnp.bfloat16)
    context = lax.map(attend, jnp.arange(length // width)).reshape(length, QUERY_HEADS * ATTN_DIM)
    result = first + jnp.dot(context, w_attn_out, preferred_element_type=jnp.float32)
    return result.astype(jnp.bfloat16)

def reference(tokens, segment_ids, norm_gain, w_mamba_in, w_ssm_param, ssm_rate, dt_bias, skip_gain, ssm_norm_gain, w_mamba_out, w_qkv, w_attn_out):
    weights = (norm_gain, w_mamba_in, w_ssm_param, ssm_rate, dt_bias, skip_gain, ssm_norm_gain, w_mamba_out, w_qkv, w_attn_out)
    rolled = tuple((jnp.roll(item, 1, axis=0) for item in weights))
    outputs = []
    for batch_index in range(tokens.shape[0]):
        section = tuple((item[batch_index] for item in rolled))
        outputs.append(micro_batch(tokens[batch_index], segment_ids[batch_index], section[0], section[1], section[2], section[3], section[4], section[5], section[6], section[7], section[8], section[9]))
    return jnp.stack(outputs, axis=0)
```

```python
import math

import jax
import jax.numpy as jnp
from jax import lax
from jax.experimental import pallas as pl
from jax.experimental.pallas import tpu as pltpu
from jax.sharding import Mesh
from jax.sharding import PartitionSpec as P


MODEL = 1024
INNER = 2048
HEAD_DIM = 64
STATE = 64
ATTN_DIM = 128
HEADS = 8
ROWS = 128
TOKENS = 512
PLANES = 8
LANES = 128
CTX = ("z", "x", "c")
epsilon = 1e-05
highest = lax.Precision.HIGHEST
f32 = jnp.float32
bf16 = jnp.bfloat16


def moved(value, axis, target):
    count = lax.axis_size(axis)
    return lax.ppermute(value, axis, [(i, target(i)) for i in range(count)])


def swapped(value, axis):
    return moved(value, axis, lambda i: 1 - i)


def ring(value, cut, after=(None, None, None)):
    found = {0: [value]}
    up = down = value
    half = PLANES // 2
    for k in range(1, half + 1):
        if k > 1 and after[k - 2] is not None:
            up, down, _ = lax.optimization_barrier((up, down, after[k - 2]))
            found[PLANES - k + 1], found[k - 1] = [up], [down]
        if k == half and cut is not None:
            up, down = up[:cut], down[cut:]
        up = moved(up, "z", lambda i: (i + 1) % PLANES)
        if k == half and cut is None:
            found[half] = [up]
            break
        down = moved(down, "z", lambda i: (i - 1) % PLANES)
        if k < half:
            found[PLANES - k], found[k] = [up], [down]
        else:
            found[half] = [up, down]
    return [part for k in range(PLANES) for part in found[k]]


smem = pl.BlockSpec(memory_space=pltpu.SMEM)
vmem = pl.BlockSpec(memory_space=pltpu.VMEM)
whole = pl.BlockSpec(memory_space=pl.ANY)


def local(kernel, outs, in_specs, scratch, flops, size, *operands, aliases=None):
    return pl.pallas_call(
        kernel,
        out_shape=tuple(jax.ShapeDtypeStruct(shape, kind) for shape, kind in outs),
        in_specs=in_specs,
        out_specs=tuple(smem if len(shape) == 1 else vmem for shape, _ in outs),
        input_output_aliases=aliases or {},
        scratch_shapes=scratch,
        cost_estimate=pl.CostEstimate(flops=flops, bytes_accessed=size, transcendentals=0),
    )(*operands)


def fetch(views, target, sems, first=0):
    copies = []
    for n, (k, view, offset, rows) in enumerate(views):
        copy = pltpu.make_async_copy(view, target(k, offset, rows), sems.at[first + n])
        copy.start()
        copies.append(copy)
    return copies


def views(refs, low, high, cut=None):
    if cut is None:
        return [(k, ref.at[low:high], 0, high - low) for k, ref in enumerate(refs)]
    found = []
    for k in range(PLANES):
        if k != PLANES // 2:
            found.append((k, refs[k + (k > PLANES // 2)].at[low:high], 0, high - low))
            continue
        if low < cut:
            end = min(high, cut)
            found.append((k, refs[k].at[low:end], 0, end - low))
        if high > cut:
            begin = max(low, cut)
            found.append((k, refs[k + 1].at[begin - cut:high - cut], begin - low, high - begin))
    return found


def placed(at_ref, scr, size):
    return lambda k, offset, rows: scr.at[
        pl.ds(pl.multiple_of(plane_of(at_ref, k) * size + offset, 16), rows)]


def plane_of(at_ref, k):
    return lax.rem(at_ref[0] + k, PLANES)


def quad_places(at_ref):
    x, c = at_ref[1], at_ref[2]
    return [2 * x + c, 2 * (1 - x) + c, 2 * x + 1 - c, 2 * (1 - x) + 1 - c]


def rows_at(block, size):
    return pl.ds(pl.multiple_of(block * size, size), size)


def split(value, parts):
    found = []
    for _ in range(parts):
        piece = value.astype(bf16)
        found.append(piece)
        value = value - piece.astype(f32)
    return found


def rms(values, gain):
    scale = lax.rsqrt(jnp.mean(values * values, axis=-1, keepdims=True) + epsilon)
    return values * scale * gain


def lane_masks():
    row = lax.broadcasted_iota(jnp.int32, (LANES, LANES), 0)
    col = lax.broadcasted_iota(jnp.int32, (LANES, LANES), 1)
    return row >= col, col < HEAD_DIM, col


def steps(raw, head_ref):
    raw = raw + head_ref[0:1, :]
    delta = jnp.maximum(raw, 0.0) + jnp.log1p(jnp.exp(-jnp.abs(raw)))
    return delta, -delta * head_ref[1:2, :]


def enter_kernel(at_ref, *refs):
    blocks, shards = refs[:4], refs[4:12]
    wout_ref, gain_ref, wprm_ref, head_ref = refs[12:16]
    u_ref, prm_ref, segc_ref, segr_ref, pack_ref = refs[16:21]
    x_scr, w_scr, n_scr, sems = refs[21:]
    places = quad_places(at_ref)
    copies = fetch([(i, blocks[i], 0, 0) for i in range(4)], lambda i, *_: x_scr.at[places[i]], sems)
    copies_w = fetch(views(shards, 0, 64), placed(at_ref, w_scr, 64), sems, 4)
    for copy in copies:
        copy.wait()
    tri, left, col = lane_masks()
    trif = tri.astype(f32)

    def normed(b, _):
        at = rows_at(b, ROWS)
        n_scr[at, :] = rms(x_scr[b, 0:ROWS, :].astype(f32), gain_ref[...].astype(f32)).astype(bf16)
        seg = x_scr[b, ROWS:ROWS + 16, 0:LANES].astype(f32)[0:1, :]
        segr_ref[:, at] = seg
        segc_ref[at, :] = jnp.transpose(jnp.broadcast_to(seg, (LANES, LANES)))
        return 0

    lax.fori_loop(0, 4, normed, 0)
    prm_ref[...] = jnp.dot(n_scr[...], wprm_ref[...], preferred_element_type=f32)
    cums, deltas = [], []
    offset = jnp.zeros((1, LANES), f32)
    for i in range(4):
        at = pl.ds(i * LANES, LANES)
        delta, log_decay = steps(prm_ref[at, LANES:2 * LANES], head_ref)
        cum = jnp.dot(trif, log_decay, precision=highest, preferred_element_type=f32) + offset
        offset = cum[LANES - 1:, :]
        cums.append(cum)
        deltas.append(delta)
    bin_t = jnp.concatenate(
        [jnp.transpose(prm_ref[pl.ds(i * LANES, LANES), 0:LANES])[STATE:, :] for i in range(4)],
        axis=1).astype(bf16)
    seg_last = segr_ref[:, TOKENS - 1:]
    for copy in copies_w:
        copy.wait()
    u_ref[...] = lax.dot_general(
        n_scr[...], w_scr[...], (((1,), (1,)), ((), ())), preferred_element_type=f32).astype(bf16)
    keeps = []
    for i in range(4):
        segc = segc_ref[pl.ds(i * LANES, LANES), :]
        keeps.append(jnp.where(segc == seg_last, jnp.exp(offset - cums[i]), 0.0) * deltas[i])
    for p in range(HEADS // 2):
        lanes = pl.ds(p * LANES, LANES)
        kept = []
        for i in range(4):
            up = u_ref[pl.ds(i * LANES, LANES), lanes].astype(f32)
            kept.append(up * jnp.where(left, keeps[i][:, 2 * p:2 * p + 1], keeps[i][:, 2 * p + 1:2 * p + 2]))
        kept = jnp.concatenate(kept, axis=0).astype(bf16)
        state = jnp.dot(bin_t, kept, preferred_element_type=f32).astype(bf16)
        pack_ref[0:32, lanes] = state[0:32]
        pack_ref[0:32, pl.ds(512 + p * LANES, LANES)] = state[32:64]
    facts = jnp.where(col[:1] < HEADS, offset, 0.0)
    facts = jnp.where(col[:1] == HEADS, seg_last, facts)
    segr = segr_ref[...]
    for v in range(4):
        count = jnp.sum(jnp.where(segr == float(v), 1.0, 0.0), axis=1, keepdims=True)
        facts = jnp.where(col[:1] == HEADS + 1 + v, count, facts)
    pieces = [piece.astype(f32) for piece in split(facts, 3)]
    rows16 = lax.broadcasted_iota(jnp.int32, (16, LANES), 0)
    fact_rows = jnp.where(rows16 == 0, pieces[0], jnp.where(rows16 == 1, pieces[1], jnp.where(rows16 == 2, pieces[2], 0.0)))
    pack_ref[32:48, :] = jnp.zeros((16, MODEL), bf16)
    pack_ref[32:48, 0:LANES] = fact_rows.astype(bf16)
    pack_ref[48:112, :] = wout_ref[...]


def space_kernel(u_ref, prm_ref, head_ref, skip_ref, segc_ref, segr_ref, y_ref, cum_ref, st_ref):
    tri, left, _ = lane_masks()
    trif = tri.astype(f32)
    st_ref[...] = jnp.zeros_like(st_ref)

    def chunk(i, carry):
        offset, seg_prev = carry
        at = rows_at(i, LANES)
        delta, log_decay = steps(prm_ref[at, LANES:2 * LANES], head_ref)
        cum = jnp.dot(trif, log_decay, precision=highest, preferred_element_type=f32)
        cum_ref[at, :] = cum + offset
        last = cum[LANES - 1:, :]
        cum_t = jnp.transpose(cum)
        delta_t = jnp.transpose(delta)
        both = prm_ref[at, 0:LANES]
        cout = both[:, :STATE].astype(bf16)
        bin_t = jnp.transpose(both)[STATE:, :].astype(bf16)
        cross = jnp.dot(cout, bin_t, preferred_element_type=f32)
        segc = segc_ref[at, :]
        segr = segr_ref[:, at]
        seg_last = segc[LANES - 1:, :]
        carried = jnp.where(segc == seg_prev, jnp.exp(cum), 0.0)
        keep = jnp.where(segc == seg_last, jnp.exp(last - cum), 0.0) * delta
        passing = jnp.where(seg_prev == seg_last, jnp.exp(last), 0.0)
        crossed = jnp.where(tri & (segc == segr), cross, 0.0)
        for p in range(HEADS // 2):
            a, b = 2 * p, 2 * p + 1
            lanes = pl.ds(p * LANES, LANES)
            up = u_ref[at, lanes]
            mix = []
            for h in (a, b):
                differ = cum[:, h:h + 1] - cum_t[h:h + 1, :]
                mix.append(jnp.exp(jnp.minimum(differ, 0.0)) * crossed * delta_t[h:h + 1, :])
            mix = jnp.concatenate(mix, axis=1).astype(bf16)
            zero = jnp.zeros_like(up)
            halves = jnp.concatenate([jnp.where(left, up, zero), jnp.where(left, zero, up)], axis=0)
            y = jnp.dot(mix, halves, preferred_element_type=f32)
            state = st_ref[:, lanes]
            y = y + jnp.dot(cout, state.astype(bf16), preferred_element_type=f32) * jnp.where(
                left, carried[:, a:a + 1], carried[:, b:b + 1])
            uf = up.astype(f32)
            y_ref[at, lanes] = y + skip_ref[:, lanes] * uf
            kept = (uf * jnp.where(left, keep[:, a:a + 1], keep[:, b:b + 1])).astype(bf16)
            pass_lane = jnp.where(left[:1], passing[:, a:a + 1], passing[:, b:b + 1])
            st_ref[:, lanes] = pass_lane * state + jnp.dot(bin_t, kept, preferred_element_type=f32)
        return offset + last, seg_last

    lax.fori_loop(0, TOKENS // LANES, chunk, (jnp.zeros((1, LANES), f32), segc_ref[0:1, :]))


def leave_kernel(at_ref, *refs):
    packs = refs[0:9]
    y_ref, cum_ref, prm_ref, segc_ref, gain_ref = refs[9:14]
    keep_ref, send_ref, start_ref, first_ref = refs[14:18]
    p_scr, w_scr, m_scr, s_scr, sems = refs[18:]
    copies = fetch(views(packs, 0, 48, 48), lambda k, *_: p_scr.at[k], sems)
    copies_w = fetch(views(packs, 48, 112, 48), placed(at_ref, w_scr, 64), sems, PLANES)
    z, x, c = at_ref[0], at_ref[1], at_ref[2]
    segc = segc_ref[...]
    seg_first = segc[0:1, 0:1]
    left = lax.broadcasted_iota(jnp.int32, (TOKENS, LANES), 1) < HEAD_DIM
    entering = jnp.where(segc == seg_first, jnp.exp(cum_ref[...]), 0.0)
    cout = prm_ref[:, 0:STATE].astype(bf16)
    for copy in copies:
        copy.wait()
    acc = jnp.zeros((1, LANES), f32)
    totals = jnp.zeros((1, LANES), f32)
    decays = [None] * PLANES
    for k in range(PLANES - 1, -1, -1):
        facts = p_scr[k, 32:48, 0:LANES].astype(f32)
        facts = facts[0:1] + facts[1:2] + facts[2:3]
        totals = totals + facts
        if k > 0:
            valid = jnp.where(z + k >= PLANES, 1.0, 0.0)
            decays[k] = jnp.where(facts[:, HEADS:HEADS + 1] == seg_first, jnp.exp(acc), 0.0) * valid
            acc = acc + facts
    below = jnp.zeros((TOKENS, LANES), f32)
    for v in range(4):
        below = below + jnp.where(segc > float(v), totals[:, HEADS + 1 + v:HEADS + 2 + v], 0.0)
    start_ref[...] = below.astype(jnp.int32)
    first_ref[0] = jnp.min(below[0:8, :]).astype(jnp.int32) // TOKENS
    squares = jnp.zeros((TOKENS, 1), f32)
    for p in range(HEADS // 2):
        lanes = pl.ds(p * LANES, LANES)
        low = jnp.zeros((32, LANES), f32)
        high = jnp.zeros((32, LANES), f32)
        for k in range(1, PLANES):
            decay = jnp.where(left[:1], decays[k][:, 2 * p:2 * p + 1], decays[k][:, 2 * p + 1:2 * p + 2])
            low = low + p_scr[k, 0:32, lanes].astype(f32) * decay
            high = high + p_scr[k, 0:32, pl.ds(512 + p * LANES, LANES)].astype(f32) * decay
        state = jnp.concatenate([low, high], axis=0).astype(bf16)
        factor = jnp.where(left, entering[:, 2 * p:2 * p + 1], entering[:, 2 * p + 1:2 * p + 2])
        mixed = y_ref[:, lanes] + jnp.dot(cout, state, preferred_element_type=f32) * factor
        squares = squares + jnp.sum(mixed * mixed, axis=1, keepdims=True)
        m_scr[:, lanes] = (mixed * gain_ref[:, lanes]).astype(bf16)
    for copy in copies_w:
        copy.wait()
    wide = lax.broadcasted_iota(jnp.int32, (ROWS, LANES), 1)
    s_scr[...] = jnp.broadcast_to(squares, (TOKENS, LANES))

    def block(b, _):
        x_ = lax.rem(b + x, 2)
        for c_, out_ref in ((c, keep_ref), (1 - c, send_ref)):
            at = rows_at(2 * x_ + c_, ROWS)
            high, low = split(s_scr[at, :], 2)
            tail = jnp.where(wide == 0, high.astype(f32), jnp.where(wide == 1, low.astype(f32), 0.0))
            part = jnp.dot(m_scr[at, :], w_scr[...], preferred_element_type=f32)
            out_ref[b, :, 0:MODEL] = part.astype(out_ref.dtype)
            out_ref[b, :, MODEL:] = tail.astype(out_ref.dtype)
        return 0

    lax.fori_loop(0, 2, block, 0)


def hidden_kernel(own_ref, other_ref, near_ref, far_ref, gain_ref, hidden_ref, first_ref):
    for b, token_ref in enumerate((own_ref, other_ref)):
        total = near_ref[b].astype(f32) + far_ref[1 - b].astype(f32)
        square = total[:, MODEL:MODEL + 1] + total[:, MODEL + 1:MODEL + 2]
        first = token_ref[0:ROWS, :].astype(f32) + total[:, 0:MODEL] * lax.rsqrt(square / INNER + epsilon)
        hidden_ref[b] = rms(first, gain_ref[...].astype(f32)).astype(bf16)
        if b == 0:
            first_ref[...] = first


def project_kernel(at_ref, *refs):
    packs = refs[0:8]
    mine_ref, theirs_ref = refs[8:10]
    q_ref, pack_ref = refs[10:12]
    w_scr, h_scr, sems = refs[12:]
    copies = fetch(views(packs, 0, 64), placed(at_ref, w_scr, 64), sems)
    x, c = at_ref[1], at_ref[2]
    for b, x_ in enumerate((x, 1 - x)):
        h_scr[rows_at(2 * x_ + c, ROWS), :] = mine_ref[b]
        h_scr[rows_at(2 * x_ + 1 - c, ROWS), :] = theirs_ref[b]
    for copy in copies:
        copy.wait()
    out = lax.dot_general(
        h_scr[...], w_scr[...], (((1,), (1,)), ((), ())), preferred_element_type=f32).astype(bf16)
    q_ref[...] = out[:, 0:256]
    pack_ref[...] = out[:, 256:512]


def attend_rows(at_ref, plane, t, k, v, q_ref, start_ref, acc_ref, stat_ref):
    tile = 256
    scale = math.log2(math.e) / math.sqrt(ATTN_DIM)
    rows = rows_at(t, tile)
    column = lax.broadcasted_iota(jnp.int32, (tile, TOKENS), 1)
    low = start_ref[rows, 0:1] - plane * TOKENS
    high = (at_ref[0] - plane) * TOKENS + t * tile + lax.broadcasted_iota(jnp.int32, (tile, 1), 0)
    seen = (column >= low) & (column <= high)
    stat = stat_ref[rows, :]
    lane = lax.broadcasted_iota(jnp.int32, (tile, LANES), 1)
    for h in range(2):
        lanes = pl.ds(h * ATTN_DIM, ATTN_DIM)
        top, total = stat[:, 2 * h:2 * h + 1], stat[:, 2 * h + 1:2 * h + 2]
        s = lax.dot_general(q_ref[rows, lanes], k, (((1,), (1,)), ((), ())), preferred_element_type=f32)
        s = jnp.where(seen, s * scale, -1e30)
        new = jnp.maximum(top, jnp.max(s, axis=1, keepdims=True))
        shift = jnp.exp2(top - new)
        p = jnp.exp2(s - new)
        total = total * shift + jnp.sum(p, axis=1, keepdims=True)
        acc_ref[rows, lanes] = acc_ref[rows, lanes] * shift + jnp.dot(
            p.astype(bf16), v, preferred_element_type=f32)
        stat = jnp.where(lane == 2 * h, new, jnp.where(lane == 2 * h + 1, total, stat))
    stat_ref[rows, :] = stat


def round_kernel(at_ref, block_ref, r_ref, up_ref, down_ref, q_ref, start_ref, acc_in, stat_in, acc_ref, stat_ref, kv_scr):
    z, first, r = at_ref[0], block_ref[0], r_ref[0]

    @pl.when(r == 0)
    def _():
        acc_ref[...] = jnp.zeros_like(acc_ref)
        lane = lax.broadcasted_iota(jnp.int32, stat_ref.shape, 1)
        stat_ref[...] = jnp.where(lane % 2 == 0, -1e29, 0.0)

    @pl.when(r > 0)
    def _():
        acc_ref[...] = acc_in[...]
        stat_ref[...] = stat_in[...]

    kv_scr[0] = up_ref[...]
    kv_scr[1] = down_ref[...]

    def part(n, _):
        side, t = n // 2, lax.rem(n, 2)
        plane = lax.rem(z + PLANES + jnp.where(side == 0, -r, r), PLANES)

        @pl.when((plane >= first) & (plane <= z) & ((side == 0) | (r > 0)))
        def _():
            attend_rows(at_ref, plane, t, kv_scr[side, :, 0:ATTN_DIM], kv_scr[side, :, ATTN_DIM:],
                        q_ref, start_ref, acc_ref, stat_ref)

        return 0

    lax.fori_loop(0, 4, part, 0)


def attend_kernel(at_ref, block_ref, *refs):
    far_ref, weights = refs[0], refs[1:9]
    q_ref, start_ref, acc_ref, stat_ref = refs[9:13]
    keep_ref, send_ref = refs[13:15]
    w_scr, c_scr, a_scr, s_scr, sems = refs[15:]
    z, first = at_ref[0], block_ref[0]
    copies_w = fetch(views(weights, 64, 96), placed(at_ref, w_scr, 32), sems)
    plane = z - PLANES // 2
    a_scr[...] = acc_ref[...]
    s_scr[...] = stat_ref[...]

    @pl.when((plane >= 0) & (plane >= first))
    def _():
        def part(t, _):
            attend_rows(at_ref, plane, t, far_ref[:, 0:ATTN_DIM], far_ref[:, ATTN_DIM:],
                        q_ref, start_ref, a_scr, s_scr)
            return 0

        lax.fori_loop(0, 2, part, 0)

    for h in range(2):
        lanes = pl.ds(h * ATTN_DIM, ATTN_DIM)
        c_scr[:, lanes] = (a_scr[:, lanes] / s_scr[:, 2 * h + 1:2 * h + 2]).astype(bf16)
    for copy in copies_w:
        copy.wait()
    x, c = at_ref[1], at_ref[2]
    for b, x_ in enumerate((x, 1 - x)):
        keep_ref[b] = jnp.dot(c_scr[rows_at(2 * x_ + c, ROWS), :], w_scr[...], preferred_element_type=f32)
        send_ref[b] = jnp.dot(
            c_scr[rows_at(2 * x_ + 1 - c, ROWS), :], w_scr[...], preferred_element_type=f32).astype(bf16)


def layer_pair(tokens, segment_ids, norm_gain, w_mamba_in, w_ssm_param, ssm_rate, dt_bias,
              skip_gain, ssm_norm_gain, w_mamba_out, w_qkv, w_attn_out):
    z, x, c = (lax.axis_index(name) for name in CTX)
    q = 2 * x + c
    at = jnp.stack([z, x, c])
    dma = pltpu.SemaphoreType.DMA

    weights = ring(jnp.transpose(w_mamba_in[0]), None)

    seg_rows = jnp.pad(segment_ids.astype(bf16), ((0, 15), (0, MODEL - ROWS)))
    own = moved(jnp.concatenate([tokens[0], seg_rows]), "blk", lambda i: (i - 1) % 8)
    own, _ = lax.optimization_barrier((own, (weights[2], weights[6])))
    other = swapped(own, "x")
    blocks = [own, other, swapped(own, "c"), swapped(other, "c")]

    heads = 4 * jnp.arange(HEADS) + q
    pick = (heads[:, None] == jnp.arange(32)[None, :]).astype(f32)
    per_head = jnp.stack([dt_bias[0], ssm_rate[0], skip_gain[0]]).astype(f32)
    per_head = jnp.dot(per_head, pick.T, precision=highest)
    head = jnp.pad(per_head[:2], ((0, 6), (0, LANES - HEADS)))
    skip = jnp.repeat(per_head[2], HEAD_DIM)[None, :]
    gain_ssm = jnp.dot(pick, ssm_norm_gain[0].reshape(32, HEAD_DIM).astype(f32), precision=highest)
    gain_ssm = gain_ssm.reshape(1, HEADS * HEAD_DIM)
    w_prm = w_ssm_param[0]
    raw = jnp.dot(w_prm[:, 2 * STATE:], pick.T.astype(bf16), preferred_element_type=f32).astype(bf16)
    w_prm = jnp.concatenate(
        [w_prm[:, STATE:2 * STATE], w_prm[:, :STATE], raw, jnp.zeros((MODEL, LANES - HEADS), bf16)], axis=1)

    order = [(s, (s % 8) * 4 + s // 8) for s in range(32)]
    qkv_slots = []
    for j in range(4):
        mine = [4 * j, 4 * j + 1, 4 * j + 2, 4 * j + 3, 16 + 2 * j, 17 + 2 * j, 24 + 2 * j, 25 + 2 * j]
        qkv_slots += [(s, k * 4 + j) for k, s in enumerate(mine)]
    turned, rows_out, _ = lax.optimization_barrier((jnp.transpose(w_qkv[0]), w_attn_out[0], weights))
    turned = lax.ppermute(turned, CTX, qkv_slots)
    rows_out = lax.ppermute(rows_out, CTX, order)
    later = jnp.concatenate([turned, rows_out])


    u, prm, segc, segr, pack = local(
        enter_kernel,
        [((TOKENS, 512), bf16), ((TOKENS, 256), f32), ((TOKENS, LANES), f32), ((1, TOKENS), f32), ((112, MODEL), bf16)],
        [smem] + [whole] * 12 + [vmem] * 4,
        [pltpu.VMEM((4, ROWS + 16, MODEL), bf16), pltpu.VMEM((512, MODEL), bf16),
         pltpu.VMEM((TOKENS, MODEL), bf16), dma((13,))],
        1 << 30, 6 << 20,
        at, *blocks, *weights, w_mamba_out[0], norm_gain[0, 0:1], w_prm, head)
    packs = ring(pack, 48)

    y, cum = local(
        space_kernel, [((TOKENS, 512), f32), ((TOKENS, LANES), f32)], [vmem] * 6,
        [pltpu.VMEM((STATE, 512), f32)], 1 << 30, 6 << 20,
        u, prm, head, skip, segc, segr)
    y, later = lax.optimization_barrier((y, later))
    keep, send, start, first_block = local(
        leave_kernel,
        [((2, ROWS, MODEL + LANES), f32), ((2, ROWS, MODEL + LANES), bf16), ((TOKENS, LANES), jnp.int32),
         ((1,), jnp.int32)],
        [smem] + [whole] * 9 + [vmem] * 5,
        [pltpu.VMEM((PLANES, 48, MODEL), bf16), pltpu.VMEM((512, MODEL), bf16),
         pltpu.VMEM((TOKENS, 512), bf16), pltpu.VMEM((TOKENS, LANES), f32), dma((16,))],
        1 << 30, 6 << 20,
        at, *packs, y, cum, prm, segc, gain_ssm)
    near = (keep + swapped(send, "c").astype(f32)).astype(bf16)
    far = swapped(near, "x")
    weights = ring(later, None, (send, near, None))
    hidden, first = local(
        hidden_kernel, [((2, ROWS, MODEL), bf16), ((ROWS, MODEL), f32)],
        [vmem] * 5, [], 1 << 20, 2 << 20,
        own, other, near, far, norm_gain[0, 1:2])

    query, pack = local(
        project_kernel, [((TOKENS, 256), bf16), ((TOKENS, 256), bf16)],
        [smem] + [whole] * 8 + [vmem] * 2,
        [pltpu.VMEM((512, MODEL), bf16), pltpu.VMEM((TOKENS, MODEL), bf16), dma((8,))],
        1 << 30, 4 << 20,
        at, *weights, hidden, swapped(hidden, "c"))

    def turn(r, carry):
        up, down, acc, stat = carry
        acc, stat = local(
            round_kernel, [((TOKENS, 256), f32), ((TOKENS, LANES), f32)],
            [smem] * 3 + [vmem] * 6, [pltpu.VMEM((2, TOKENS, 256), bf16)],
            1 << 30, 3 << 20,
            at, first_block, r.reshape(1), up, down, query, start, acc, stat, aliases={7: 0, 8: 1})
        up = moved(up, "z", lambda i: (i + 1) % PLANES)
        down = moved(down, "z", lambda i: (i - 1) % PLANES)
        return up, down, acc, stat

    empty = (jnp.zeros((TOKENS, 256), f32), jnp.zeros((TOKENS, LANES), f32))
    far, _, acc, stat = lax.fori_loop(0, PLANES // 2, turn, (pack, pack, *empty))
    keep, send = local(
        attend_kernel, [((2, ROWS, MODEL), f32), ((2, ROWS, MODEL), bf16)],
        [smem, smem, vmem] + [whole] * 8 + [vmem] * 4,
        [pltpu.VMEM((256, MODEL), bf16), pltpu.VMEM((TOKENS, 256), bf16),
         pltpu.VMEM((TOKENS, 256), f32), pltpu.VMEM((TOKENS, LANES), f32), dma((8,))],
        1 << 30, 6 << 20,
        at, first_block, far, *weights, query, start, acc, stat)
    got = swapped(send, "c").astype(f32)
    mine = (first + keep[0] + got[0]).astype(bf16)
    send = (keep[1] + got[1]).astype(bf16)
    place = lambda i, f: ((i // 4 + 1) % 8) * 4 + f(i % 4)
    straight = [(i, place(i, lambda k: k)) for i in range(32)]
    cross = [(i, place(i, lambda k: k ^ 2)) for i in range(32)]
    mine = lax.ppermute(mine, ("blk", "x", "c"), straight)
    theirs = lax.ppermute(send, ("blk", "x", "c"), cross)
    return (mine.astype(f32) + theirs.astype(f32)).astype(bf16)[None]


def solution(mesh):
    finer = Mesh(mesh.devices.reshape(8, PLANES, 2, 2), ("blk", *CTX))
    rows = lambda *spec: P("blk", *spec)
    in_specs = (
        rows(CTX, None), rows(CTX), rows(None, None), rows(None, CTX), rows(None, None), rows(None),
        rows(None), rows(None), rows(None), rows(CTX, None), rows(None, CTX), rows(CTX, None),
    )
    return jax.shard_map(
        layer_pair, mesh=finer, in_specs=in_specs, out_specs=rows(CTX, None), check_vma=False)
```

```python
import math

import jax
import jax.numpy as jnp
from jax import lax
from jax.experimental import pallas as pl
from jax.experimental.pallas import tpu as pltpu
from jax.sharding import Mesh
from jax.sharding import PartitionSpec as P


MODEL = 1024
INNER = 2048
HEAD_DIM = 64
STATE = 64
ATTN_DIM = 128
HEADS = 8
ROWS = 128
TOKENS = 512
PLANES = 8
LANES = 128
CTX = ("z", "x", "c")
epsilon = 1e-05
highest = lax.Precision.HIGHEST
f32 = jnp.float32
bf16 = jnp.bfloat16


def moved(value, axis, target):
    count = lax.axis_size(axis)
    return lax.ppermute(value, axis, [(i, target(i)) for i in range(count)])


def swapped(value, axis):
    return moved(value, axis, lambda i: 1 - i)


def ring(value, cut, after=(None, None, None)):
    found = {0: [value]}
    up = down = value
    half = PLANES // 2
    for k in range(1, half + 1):
        if k > 1 and after[k - 2] is not None:
            up, down, _ = lax.optimization_barrier((up, down, after[k - 2]))
            found[PLANES - k + 1], found[k - 1] = [up], [down]
        if k == half and cut is not None:
            up, down = up[:cut], down[cut:]
        up = moved(up, "z", lambda i: (i + 1) % PLANES)
        if k == half and cut is None:
            found[half] = [up]
            break
        down = moved(down, "z", lambda i: (i - 1) % PLANES)
        if k < half:
            found[PLANES - k], found[k] = [up], [down]
        else:
            found[half] = [up, down]
    return [part for k in range(PLANES) for part in found[k]]


smem = pl.BlockSpec(memory_space=pltpu.SMEM)
vmem = pl.BlockSpec(memory_space=pltpu.VMEM)
whole = pl.BlockSpec(memory_space=pl.ANY)


def local(kernel, outs, in_specs, scratch, flops, size, *operands, aliases=None):
    return pl.pallas_call(
        kernel,
        out_shape=tuple(jax.ShapeDtypeStruct(shape, kind) for shape, kind in outs),
        in_specs=in_specs,
        out_specs=tuple(smem if len(shape) == 1 else vmem for shape, _ in outs),
        input_output_aliases=aliases or {},
        scratch_shapes=scratch,
        cost_estimate=pl.CostEstimate(flops=flops, bytes_accessed=size, transcendentals=0),
    )(*operands)


def fetch(views, target, sems, first=0):
    copies = []
    for n, (k, view, offset, rows) in enumerate(views):
        copy = pltpu.make_async_copy(view, target(k, offset, rows), sems.at[first + n])
        copy.start()
        copies.append(copy)
    return copies


def views(refs, low, high, cut=None):
    if cut is None:
        return [(k, ref.at[low:high], 0, high - low) for k, ref in enumerate(refs)]
    found = []
    for k in range(PLANES):
        if k != PLANES // 2:
            found.append((k, refs[k + (k > PLANES // 2)].at[low:high], 0, high - low))
            continue
        if low < cut:
            end = min(high, cut)
            found.append((k, refs[k].at[low:end], 0, end - low))
        if high > cut:
            begin = max(low, cut)
            found.append((k, refs[k + 1].at[begin - cut:high - cut], begin - low, high - begin))
    return found


def placed(at_ref, scr, size):
    return lambda k, offset, rows: scr.at[
        pl.ds(pl.multiple_of(plane_of(at_ref, k) * size + offset, 16), rows)]


def plane_of(at_ref, k):
    return lax.rem(at_ref[0] + k, PLANES)


def quad_places(at_ref):
    x, c = at_ref[1], at_ref[2]
    return [2 * x + c, 2 * (1 - x) + c, 2 * x + 1 - c, 2 * (1 - x) + 1 - c]


def rows_at(block, size):
    return pl.ds(pl.multiple_of(block * size, size), size)


def split(value, parts):
    found = []
    for _ in range(parts):
        piece = value.astype(bf16)
        found.append(piece)
        value = value - piece.astype(f32)
    return found


def rms(values, gain):
    scale = lax.rsqrt(jnp.mean(values * values, axis=-1, keepdims=True) + epsilon)
    return values * scale * gain


def lane_masks():
    row = lax.broadcasted_iota(jnp.int32, (LANES, LANES), 0)
    col = lax.broadcasted_iota(jnp.int32, (LANES, LANES), 1)
    return row >= col, col < HEAD_DIM, col


def steps(raw, head_ref):
    raw = raw + head_ref[0:1, :]
    delta = jnp.maximum(raw, 0.0) + jnp.log1p(jnp.exp(-jnp.abs(raw)))
    return delta, -delta * head_ref[1:2, :]


def enter_kernel(at_ref, *refs):
    blocks, shards = refs[:4], refs[4:12]
    wout_ref, gain_ref, wprm_ref, head_ref = refs[12:16]
    u_ref, prm_ref, segc_ref, segr_ref, pack_ref = refs[16:21]
    x_scr, w_scr, n_scr, sems = refs[21:]
    places = quad_places(at_ref)
    copies = fetch([(i, blocks[i], 0, 0) for i in range(4)], lambda i, *_: x_scr.at[places[i]], sems)
    copies_w = fetch(views(shards, 0, 64), placed(at_ref, w_scr, 64), sems, 4)
    for copy in copies:
        copy.wait()
    tri, left, col = lane_masks()
    trif = tri.astype(f32)

    def normed(b, _):
        at = rows_at(b, ROWS)
        n_scr[at, :] = rms(x_scr[b, 0:ROWS, :].astype(f32), gain_ref[...].astype(f32)).astype(bf16)
        seg = x_scr[b, ROWS:ROWS + 16, 0:LANES].astype(f32)[0:1, :]
        segr_ref[:, at] = seg
        segc_ref[at, :] = jnp.transpose(jnp.broadcast_to(seg, (LANES, LANES)))
        return 0

    lax.fori_loop(0, 4, normed, 0)
    prm_ref[...] = jnp.dot(n_scr[...], wprm_ref[...], preferred_element_type=f32)
    cums, deltas = [], []
    offset = jnp.zeros((1, LANES), f32)
    for i in range(4):
        at = pl.ds(i * LANES, LANES)
        delta, log_decay = steps(prm_ref[at, LANES:2 * LANES], head_ref)
        cum = jnp.dot(trif, log_decay, precision=highest, preferred_element_type=f32) + offset
        offset = cum[LANES - 1:, :]
        cums.append(cum)
        deltas.append(delta)
    bin_t = jnp.concatenate(
        [jnp.transpose(prm_ref[pl.ds(i * LANES, LANES), 0:LANES])[STATE:, :] for i in range(4)],
        axis=1).astype(bf16)
    seg_last = segr_ref[:, TOKENS - 1:]
    for copy in copies_w:
        copy.wait()
    u_ref[...] = lax.dot_general(
        n_scr[...], w_scr[...], (((1,), (1,)), ((), ())), preferred_element_type=f32).astype(bf16)
    keeps = []
    for i in range(4):
        segc = segc_ref[pl.ds(i * LANES, LANES), :]
        keeps.append(jnp.where(segc == seg_last, jnp.exp(offset - cums[i]), 0.0) * deltas[i])
    for p in range(HEADS // 2):
        lanes = pl.ds(p * LANES, LANES)
        kept = []
        for i in range(4):
            up = u_ref[pl.ds(i * LANES, LANES), lanes].astype(f32)
            kept.append(up * jnp.where(left, keeps[i][:, 2 * p:2 * p + 1], keeps[i][:, 2 * p + 1:2 * p + 2]))
        kept = jnp.concatenate(kept, axis=0).astype(bf16)
        state = jnp.dot(bin_t, kept, preferred_element_type=f32).astype(bf16)
        pack_ref[0:32, lanes] = state[0:32]
        pack_ref[0:32, pl.ds(512 + p * LANES, LANES)] = state[32:64]
    facts = jnp.where(col[:1] < HEADS, offset, 0.0)
    facts = jnp.where(col[:1] == HEADS, seg_last, facts)
    segr = segr_ref[...]
    for v in range(4):
        count = jnp.sum(jnp.where(segr == float(v), 1.0, 0.0), axis=1, keepdims=True)
        facts = jnp.where(col[:1] == HEADS + 1 + v, count, facts)
    pieces = [piece.astype(f32) for piece in split(facts, 3)]
    rows16 = lax.broadcasted_iota(jnp.int32, (16, LANES), 0)
    fact_rows = jnp.where(rows16 == 0, pieces[0], jnp.where(rows16 == 1, pieces[1], jnp.where(rows16 == 2, pieces[2], 0.0)))
    pack_ref[32:48, :] = jnp.zeros((16, MODEL), bf16)
    pack_ref[32:48, 0:LANES] = fact_rows.astype(bf16)
    pack_ref[48:112, :] = wout_ref[...]


def space_kernel(u_ref, prm_ref, head_ref, skip_ref, segc_ref, segr_ref, y_ref, cum_ref, st_ref):
    tri, left, _ = lane_masks()
    trif = tri.astype(f32)
    st_ref[...] = jnp.zeros_like(st_ref)

    def chunk(i, carry):
        offset, seg_prev = carry
        at = rows_at(i, LANES)
        delta, log_decay = steps(prm_ref[at, LANES:2 * LANES], head_ref)
        cum = jnp.dot(trif, log_decay, precision=highest, preferred_element_type=f32)
        cum_ref[at, :] = cum + offset
        last = cum[LANES - 1:, :]
        cum_t = jnp.transpose(cum)
        delta_t = jnp.transpose(delta)
        both = prm_ref[at, 0:LANES]
        cout = both[:, :STATE].astype(bf16)
        bin_t = jnp.transpose(both)[STATE:, :].astype(bf16)
        cross = jnp.dot(cout, bin_t, preferred_element_type=f32)
        segc = segc_ref[at, :]
        segr = segr_ref[:, at]
        seg_last = segc[LANES - 1:, :]
        carried = jnp.where(segc == seg_prev, jnp.exp(cum), 0.0)
        keep = jnp.where(segc == seg_last, jnp.exp(last - cum), 0.0) * delta
        passing = jnp.where(seg_prev == seg_last, jnp.exp(last), 0.0)
        crossed = jnp.where(tri & (segc == segr), cross, 0.0)
        for p in range(HEADS // 2):
            a, b = 2 * p, 2 * p + 1
            lanes = pl.ds(p * LANES, LANES)
            up = u_ref[at, lanes]
            mix = []
            for h in (a, b):
                differ = cum[:, h:h + 1] - cum_t[h:h + 1, :]
                mix.append(jnp.exp(jnp.minimum(differ, 0.0)) * crossed * delta_t[h:h + 1, :])
            mix = jnp.concatenate(mix, axis=1).astype(bf16)
            zero = jnp.zeros_like(up)
            halves = jnp.concatenate([jnp.where(left, up, zero), jnp.where(left, zero, up)], axis=0)
            y = jnp.dot(mix, halves, preferred_element_type=f32)
            state = st_ref[:, lanes]
            y = y + jnp.dot(cout, state.astype(bf16), preferred_element_type=f32) * jnp.where(
                left, carried[:, a:a + 1], carried[:, b:b + 1])
            uf = up.astype(f32)
            y_ref[at, lanes] = y + skip_ref[:, lanes] * uf
            kept = (uf * jnp.where(left, keep[:, a:a + 1], keep[:, b:b + 1])).astype(bf16)
            pass_lane = jnp.where(left[:1], passing[:, a:a + 1], passing[:, b:b + 1])
            st_ref[:, lanes] = pass_lane * state + jnp.dot(bin_t, kept, preferred_element_type=f32)
        return offset + last, seg_last

    lax.fori_loop(0, TOKENS // LANES, chunk, (jnp.zeros((1, LANES), f32), segc_ref[0:1, :]))


def leave_kernel(at_ref, *refs):
    packs = refs[0:9]
    y_ref, cum_ref, prm_ref, segc_ref, gain_ref = refs[9:14]
    keep_ref, send_ref, start_ref, first_ref = refs[14:18]
    p_scr, w_scr, m_scr, s_scr, sems = refs[18:]
    copies = fetch(views(packs, 0, 48, 48), lambda k, *_: p_scr.at[k], sems)
    copies_w = fetch(views(packs, 48, 112, 48), placed(at_ref, w_scr, 64), sems, PLANES)
    z, x, c = at_ref[0], at_ref[1], at_ref[2]
    segc = segc_ref[...]
    seg_first = segc[0:1, 0:1]
    left = lax.broadcasted_iota(jnp.int32, (TOKENS, LANES), 1) < HEAD_DIM
    entering = jnp.where(segc == seg_first, jnp.exp(cum_ref[...]), 0.0)
    cout = prm_ref[:, 0:STATE].astype(bf16)
    for copy in copies:
        copy.wait()
    acc = jnp.zeros((1, LANES), f32)
    totals = jnp.zeros((1, LANES), f32)
    decays = [None] * PLANES
    for k in range(PLANES - 1, -1, -1):
        facts = p_scr[k, 32:48, 0:LANES].astype(f32)
        facts = facts[0:1] + facts[1:2] + facts[2:3]
        totals = totals + facts
        if k > 0:
            valid = jnp.where(z + k >= PLANES, 1.0, 0.0)
            decays[k] = jnp.where(facts[:, HEADS:HEADS + 1] == seg_first, jnp.exp(acc), 0.0) * valid
            acc = acc + facts
    below = jnp.zeros((TOKENS, LANES), f32)
    for v in range(4):
        below = below + jnp.where(segc > float(v), totals[:, HEADS + 1 + v:HEADS + 2 + v], 0.0)
    start_ref[...] = below.astype(jnp.int32)
    first_ref[0] = jnp.min(below[0:8, :]).astype(jnp.int32) // TOKENS
    squares = jnp.zeros((TOKENS, 1), f32)
    for p in range(HEADS // 2):
        lanes = pl.ds(p * LANES, LANES)
        low = jnp.zeros((32, LANES), f32)
        high = jnp.zeros((32, LANES), f32)
        for k in range(1, PLANES):
            decay = jnp.where(left[:1], decays[k][:, 2 * p:2 * p + 1], decays[k][:, 2 * p + 1:2 * p + 2])
            low = low + p_scr[k, 0:32, lanes].astype(f32) * decay
            high = high + p_scr[k, 0:32, pl.ds(512 + p * LANES, LANES)].astype(f32) * decay
        state = jnp.concatenate([low, high], axis=0).astype(bf16)
        factor = jnp.where(left, entering[:, 2 * p:2 * p + 1], entering[:, 2 * p + 1:2 * p + 2])
        mixed = y_ref[:, lanes] + jnp.dot(cout, state, preferred_element_type=f32) * factor
        squares = squares + jnp.sum(mixed * mixed, axis=1, keepdims=True)
        m_scr[:, lanes] = (mixed * gain_ref[:, lanes]).astype(bf16)
    for copy in copies_w:
        copy.wait()
    wide = lax.broadcasted_iota(jnp.int32, (ROWS, LANES), 1)
    s_scr[...] = jnp.broadcast_to(squares, (TOKENS, LANES))

    def block(b, _):
        x_ = lax.rem(b + x, 2)
        for c_, out_ref in ((c, keep_ref), (1 - c, send_ref)):
            at = rows_at(2 * x_ + c_, ROWS)
            high, low = split(s_scr[at, :], 2)
            tail = jnp.where(wide == 0, high.astype(f32), jnp.where(wide == 1, low.astype(f32), 0.0))
            part = jnp.dot(m_scr[at, :], w_scr[...], preferred_element_type=f32)
            out_ref[b, :, 0:MODEL] = part.astype(out_ref.dtype)
            out_ref[b, :, MODEL:] = tail.astype(out_ref.dtype)
        return 0

    lax.fori_loop(0, 2, block, 0)


def hidden_kernel(own_ref, other_ref, near_ref, far_ref, gain_ref, hidden_ref, first_ref):
    for b, token_ref in enumerate((own_ref, other_ref)):
        total = near_ref[b].astype(f32) + far_ref[1 - b].astype(f32)
        square = total[:, MODEL:MODEL + 1] + total[:, MODEL + 1:MODEL + 2]
        first = token_ref[0:ROWS, :].astype(f32) + total[:, 0:MODEL] * lax.rsqrt(square / INNER + epsilon)
        hidden_ref[b] = rms(first, gain_ref[...].astype(f32)).astype(bf16)
        if b == 0:
            first_ref[...] = first


def project_kernel(at_ref, *refs):
    packs = refs[0:9]
    mine_ref, theirs_ref = refs[9:11]
    q_ref, pack_ref = refs[11:13]
    w_scr, h_scr, sems = refs[13:]
    copies = fetch(views(packs, 0, 64, 48), placed(at_ref, w_scr, 64), sems)
    x, c = at_ref[1], at_ref[2]
    for b, x_ in enumerate((x, 1 - x)):
        h_scr[rows_at(2 * x_ + c, ROWS), :] = mine_ref[b]
        h_scr[rows_at(2 * x_ + 1 - c, ROWS), :] = theirs_ref[b]
    for copy in copies:
        copy.wait()
    out = lax.dot_general(
        h_scr[...], w_scr[...], (((1,), (1,)), ((), ())), preferred_element_type=f32).astype(bf16)
    q_ref[...] = out[:, 0:256]
    pack_ref[...] = out[:, 256:512]


def attend_rows(at_ref, plane, t, k, v, q_ref, start_ref, acc_ref, stat_ref):
    tile = 256
    scale = math.log2(math.e) / math.sqrt(ATTN_DIM)
    rows = rows_at(t, tile)
    column = lax.broadcasted_iota(jnp.int32, (tile, TOKENS), 1)
    low = start_ref[rows, 0:1] - plane * TOKENS
    high = (at_ref[0] - plane) * TOKENS + t * tile + lax.broadcasted_iota(jnp.int32, (tile, 1), 0)
    seen = (column >= low) & (column <= high)
    stat = stat_ref[rows, :]
    lane = lax.broadcasted_iota(jnp.int32, (tile, LANES), 1)
    for h in range(2):
        lanes = pl.ds(h * ATTN_DIM, ATTN_DIM)
        top, total = stat[:, 2 * h:2 * h + 1], stat[:, 2 * h + 1:2 * h + 2]
        s = lax.dot_general(q_ref[rows, lanes], k, (((1,), (1,)), ((), ())), preferred_element_type=f32)
        s = jnp.where(seen, s * scale, -1e30)
        new = jnp.maximum(top, jnp.max(s, axis=1, keepdims=True))
        shift = jnp.exp2(top - new)
        p = jnp.exp2(s - new)
        total = total * shift + jnp.sum(p, axis=1, keepdims=True)
        acc_ref[rows, lanes] = acc_ref[rows, lanes] * shift + jnp.dot(
            p.astype(bf16), v, preferred_element_type=f32)
        stat = jnp.where(lane == 2 * h, new, jnp.where(lane == 2 * h + 1, total, stat))
    stat_ref[rows, :] = stat


def round_kernel(at_ref, block_ref, r_ref, up_ref, down_ref, q_ref, start_ref, acc_in, stat_in, acc_ref, stat_ref, kv_scr):
    z, first, r = at_ref[0], block_ref[0], r_ref[0]

    @pl.when(r == 0)
    def _():
        acc_ref[...] = jnp.zeros_like(acc_ref)
        lane = lax.broadcasted_iota(jnp.int32, stat_ref.shape, 1)
        stat_ref[...] = jnp.where(lane % 2 == 0, -1e29, 0.0)

    @pl.when(r > 0)
    def _():
        acc_ref[...] = acc_in[...]
        stat_ref[...] = stat_in[...]

    kv_scr[0] = up_ref[...]
    kv_scr[1] = down_ref[...]

    def part(n, _):
        side, t = n // 2, lax.rem(n, 2)
        plane = lax.rem(z + PLANES + jnp.where(side == 0, -r, r), PLANES)

        @pl.when((plane >= first) & (plane <= z) & ((side == 0) | (r > 0)))
        def _():
            attend_rows(at_ref, plane, t, kv_scr[side, :, 0:ATTN_DIM], kv_scr[side, :, ATTN_DIM:],
                        q_ref, start_ref, acc_ref, stat_ref)

        return 0

    lax.fori_loop(0, 4, part, 0)


def attend_kernel(at_ref, block_ref, *refs):
    far_ref, weights = refs[0], refs[1:10]
    q_ref, start_ref, acc_ref, stat_ref = refs[10:14]
    keep_ref, send_ref = refs[14:16]
    w_scr, c_scr, a_scr, s_scr, sems = refs[16:]
    z, first = at_ref[0], block_ref[0]
    copies_w = fetch(views(weights, 64, 96, 48), placed(at_ref, w_scr, 32), sems)
    plane = z - PLANES // 2
    a_scr[...] = acc_ref[...]
    s_scr[...] = stat_ref[...]

    @pl.when((plane >= 0) & (plane >= first))
    def _():
        def part(t, _):
            attend_rows(at_ref, plane, t, far_ref[:, 0:ATTN_DIM], far_ref[:, ATTN_DIM:],
                        q_ref, start_ref, a_scr, s_scr)
            return 0

        lax.fori_loop(0, 2, part, 0)

    for h in range(2):
        lanes = pl.ds(h * ATTN_DIM, ATTN_DIM)
        c_scr[:, lanes] = (a_scr[:, lanes] / s_scr[:, 2 * h + 1:2 * h + 2]).astype(bf16)
    for copy in copies_w:
        copy.wait()
    x, c = at_ref[1], at_ref[2]
    for b, x_ in enumerate((x, 1 - x)):
        keep_ref[b] = jnp.dot(c_scr[rows_at(2 * x_ + c, ROWS), :], w_scr[...], preferred_element_type=f32)
        send_ref[b] = jnp.dot(
            c_scr[rows_at(2 * x_ + 1 - c, ROWS), :], w_scr[...], preferred_element_type=f32).astype(bf16)


def layer_pair(tokens, segment_ids, norm_gain, w_mamba_in, w_ssm_param, ssm_rate, dt_bias,
              skip_gain, ssm_norm_gain, w_mamba_out, w_qkv, w_attn_out):
    z, x, c = (lax.axis_index(name) for name in CTX)
    q = 2 * x + c
    at = jnp.stack([z, x, c])
    dma = pltpu.SemaphoreType.DMA

    weights = ring(jnp.transpose(w_mamba_in[0]), None)

    seg_rows = jnp.pad(segment_ids.astype(bf16), ((0, 15), (0, MODEL - ROWS)))
    own = moved(jnp.concatenate([tokens[0], seg_rows]), "blk", lambda i: (i - 1) % 8)
    own, _ = lax.optimization_barrier((own, (weights[2], weights[6])))
    other = swapped(own, "x")
    blocks = [own, other, swapped(own, "c"), swapped(other, "c")]

    heads = 4 * jnp.arange(HEADS) + q
    pick = (heads[:, None] == jnp.arange(32)[None, :]).astype(f32)
    per_head = jnp.stack([dt_bias[0], ssm_rate[0], skip_gain[0]]).astype(f32)
    per_head = jnp.dot(per_head, pick.T, precision=highest)
    head = jnp.pad(per_head[:2], ((0, 6), (0, LANES - HEADS)))
    skip = jnp.repeat(per_head[2], HEAD_DIM)[None, :]
    gain_ssm = jnp.dot(pick, ssm_norm_gain[0].reshape(32, HEAD_DIM).astype(f32), precision=highest)
    gain_ssm = gain_ssm.reshape(1, HEADS * HEAD_DIM)
    w_prm = w_ssm_param[0]
    raw = jnp.dot(w_prm[:, 2 * STATE:], pick.T.astype(bf16), preferred_element_type=f32).astype(bf16)
    w_prm = jnp.concatenate(
        [w_prm[:, STATE:2 * STATE], w_prm[:, :STATE], raw, jnp.zeros((MODEL, LANES - HEADS), bf16)], axis=1)

    order = [(s, (s % 8) * 4 + s // 8) for s in range(32)]
    qkv_slots = []
    for j in range(4):
        mine = [4 * j, 4 * j + 1, 4 * j + 2, 4 * j + 3, 16 + 2 * j, 17 + 2 * j, 24 + 2 * j, 25 + 2 * j]
        qkv_slots += [(s, k * 4 + j) for k, s in enumerate(mine)]
    turned = lax.ppermute(jnp.transpose(w_qkv[0]), CTX, qkv_slots)
    rows_out = lax.ppermute(w_attn_out[0], CTX, order)
    later = jnp.concatenate([turned, rows_out])


    u, prm, segc, segr, pack = local(
        enter_kernel,
        [((TOKENS, 512), bf16), ((TOKENS, 256), f32), ((TOKENS, LANES), f32), ((1, TOKENS), f32), ((112, MODEL), bf16)],
        [smem] + [whole] * 12 + [vmem] * 4,
        [pltpu.VMEM((4, ROWS + 16, MODEL), bf16), pltpu.VMEM((512, MODEL), bf16),
         pltpu.VMEM((TOKENS, MODEL), bf16), dma((13,))],
        1 << 30, 6 << 20,
        at, *blocks, *weights, w_mamba_out[0], norm_gain[0, 0:1], w_prm, head)
    packs = ring(pack, 48)

    y, cum = local(
        space_kernel, [((TOKENS, 512), f32), ((TOKENS, LANES), f32)], [vmem] * 6,
        [pltpu.VMEM((STATE, 512), f32)], 1 << 30, 6 << 20,
        u, prm, head, skip, segc, segr)
    keep, send, start, first_block = local(
        leave_kernel,
        [((2, ROWS, MODEL + LANES), f32), ((2, ROWS, MODEL + LANES), bf16), ((TOKENS, LANES), jnp.int32),
         ((1,), jnp.int32)],
        [smem] + [whole] * 9 + [vmem] * 5,
        [pltpu.VMEM((PLANES, 48, MODEL), bf16), pltpu.VMEM((512, MODEL), bf16),
         pltpu.VMEM((TOKENS, 512), bf16), pltpu.VMEM((TOKENS, LANES), f32), dma((16,))],
        1 << 30, 6 << 20,
        at, *packs, y, cum, prm, segc, gain_ssm)
    near = swapped(send, "c")
    near = (keep + near.astype(f32)).astype(bf16)
    far = swapped(near, "x")
    weights = ring(later, 48, (None, near, None))
    hidden, first = local(
        hidden_kernel, [((2, ROWS, MODEL), bf16), ((ROWS, MODEL), f32)],
        [vmem] * 5, [], 1 << 20, 2 << 20,
        own, other, near, far, norm_gain[0, 1:2])

    query, pack = local(
        project_kernel, [((TOKENS, 256), bf16), ((TOKENS, 256), bf16)],
        [smem] + [whole] * 9 + [vmem] * 2,
        [pltpu.VMEM((512, MODEL), bf16), pltpu.VMEM((TOKENS, MODEL), bf16), dma((9,))],
        1 << 30, 4 << 20,
        at, *weights, hidden, swapped(hidden, "c"))

    def turn(r, carry):
        up, down, acc, stat = carry
        acc, stat = local(
            round_kernel, [((TOKENS, 256), f32), ((TOKENS, LANES), f32)],
            [smem] * 3 + [vmem] * 6, [pltpu.VMEM((2, TOKENS, 256), bf16)],
            1 << 30, 3 << 20,
            at, first_block, r.reshape(1), up, down, query, start, acc, stat, aliases={7: 0, 8: 1})
        up = moved(up, "z", lambda i: (i + 1) % PLANES)
        down = moved(down, "z", lambda i: (i - 1) % PLANES)
        return up, down, acc, stat

    empty = (jnp.zeros((TOKENS, 256), f32), jnp.zeros((TOKENS, LANES), f32))
    far, _, acc, stat = lax.fori_loop(0, PLANES // 2, turn, (pack, pack, *empty))
    keep, send = local(
        attend_kernel, [((2, ROWS, MODEL), f32), ((2, ROWS, MODEL), bf16)],
        [smem, smem, vmem] + [whole] * 9 + [vmem] * 4,
        [pltpu.VMEM((256, MODEL), bf16), pltpu.VMEM((TOKENS, 256), bf16),
         pltpu.VMEM((TOKENS, 256), f32), pltpu.VMEM((TOKENS, LANES), f32), dma((8,))],
        1 << 30, 6 << 20,
        at, first_block, far, *weights, query, start, acc, stat)
    got = swapped(send, "c").astype(f32)
    mine = (first + keep[0] + got[0]).astype(bf16)
    send = (keep[1] + got[1]).astype(bf16)
    place = lambda i, f: ((i // 4 + 1) % 8) * 4 + f(i % 4)
    straight = [(i, place(i, lambda k: k)) for i in range(32)]
    cross = [(i, place(i, lambda k: k ^ 2)) for i in range(32)]
    mine = lax.ppermute(mine, ("blk", "x", "c"), straight)
    theirs = lax.ppermute(send, ("blk", "x", "c"), cross)
    return (mine.astype(f32) + theirs.astype(f32)).astype(bf16)[None]


def solution(mesh):
    finer = Mesh(mesh.devices.reshape(8, PLANES, 2, 2), ("blk", *CTX))
    rows = lambda *spec: P("blk", *spec)
    in_specs = (
        rows(CTX, None), rows(CTX), rows(None, None), rows(None, CTX), rows(None, None), rows(None),
        rows(None), rows(None), rows(None), rows(CTX, None), rows(None, CTX), rows(CTX, None),
    )
    return jax.shard_map(
        layer_pair, mesh=finer, in_specs=in_specs, out_specs=rows(CTX, None), check_vma=False)
```
